32 devices in a mesh: space: 16 (over z, y, core), band: 2 (over x).
Axes of the slice: x: 2, y: 2, z: 4, core: 2. Of those that a mesh axis runs over, the one named last changes fastest.
Arguments:
- orbitals: float32 [48, 16, 8, 16, 128], P('band', 'space'), may hold values from -100 to 100
- potential: float32 [16, 8, 16, 128], P('space'), may hold values from 0.5 to 4
Outputs:
- basis: float32 [48, 16, 8, 16, 128], P('band', 'space')
- factor: float32 [48, 48], replicated
The draws below stay inside these ranges and needn't reach their ends.
All inputs are finite; a program needn't handle non-finite values.
Results may differ from the reference program's by a relative error of at most 0.0003.
Values sent between devices are 32-bit elements; how exact they have to be, the bound alone decides.
A program may use at most 64 MiB of HBM per device.

```python
import math
import jax
import jax.numpy as jnp
from jax import lax

NORB = 48
DEG = 4
CX = 8
CY = 16
CZ = 128
TILES = 16
TX = 1


def draw_orbitals(key, part):
    shape = (NORB, TILES, CX, CY, CZ)
    field_shape = (1, TILES, CX, CY, CZ)
    key_base, key_cells, key_orbs, key_common, key_weights, key_spread = jax.random.split(key, 6)
    tile_position = jnp.arange(TILES, dtype=jnp.float32) / max(TILES - 1, 1)
    tile_scale = (3.0 ** tile_position).reshape(1, TILES, 1, 1, 1)
    cell_scale = 10.0 ** jax.random.uniform(key_cells, field_shape, jnp.float32)
    orbital_scale = 10.0 ** jax.random.uniform(key_orbs, (NORB, 1, 1, 1, 1), jnp.float32)
    weights = jax.random.uniform(key_weights, (NORB, 1, 1, 1, 1), jnp.float32, 0.6, 1.4)
    spread = jax.random.uniform(key_spread, (NORB, 1, 1, 1, 1), jnp.float32)
    spread = (spread - jnp.min(spread)) / (jnp.max(spread) - jnp.min(spread))
    lowest = 0.012
    own_weight = lowest ** (1.0 - spread)
    base = jnp.clip(jax.random.normal(key_base, shape, jnp.float32), -4.0, 4.0)
    common = jnp.clip(jax.random.normal(key_common, field_shape, jnp.float32), -4.0, 4.0)
    mixed = weights * common + own_weight * base
    return (0.025 * mixed * cell_scale * orbital_scale * tile_scale).astype(jnp.float32)


def block_scale(stream_key, shape, shards, smallest, largest):
    level = 1.0
    for axis_at, parts in shards:
        heights = jax.random.uniform(jax.random.fold_in(jax.random.fold_in(stream_key, 6), axis_at), (parts,), jnp.float32, smallest / len(shards), largest / len(shards))
        level = level * jnp.repeat(jnp.exp(heights), shape[axis_at] // parts).reshape((-1,) + (1,) * (len(shape) - 1 - axis_at))
    return level


def setup_inputs(seed: int = 0) -> dict:
    splits = jax.random.split(jax.random.key(seed), 3)
    return {
        "orbitals": draw_orbitals(jax.random.fold_in(splits[2], 71), 0),
        "potential": jnp.clip(jnp.exp(math.log(4.0) - 2.0794415 * jax.random.uniform(splits[1], (TILES, CX, CY, CZ), jnp.float32) ** block_scale(splits[1], (TILES, CX, CY, CZ), ((0, 16),), -0.2, 0.2)), 0.5, 4.0),
    }


coefficients = (-205.0 / 72.0, 8.0 / 5.0, -1.0 / 5.0, 8.0 / 315.0, -1.0 / 560.0)
centre_value = 9.25
half_range = 4.75
filter_scale = 1.0 / 32.0

def to_grid(tiles):
    shaped = tiles.reshape(TX, 4, 4, CX, CY, CZ)
    return shaped.transpose(0, 3, 1, 4, 2, 5).reshape(TX * CX, 4 * CY, 4 * CZ)

def from_grid(grid_values):
    shaped = grid_values.reshape(TX, CX, 4, CY, 4, CZ)
    return shaped.transpose(0, 2, 4, 1, 3, 5).reshape(TILES, CX, CY, CZ)

def laplacian(values):
    total = 3.0 * coefficients[0] * values
    for axis_dim in range(3):
        widths = [(0, 0), (0, 0), (0, 0)]
        widths[axis_dim] = (4, 4)
        padded = jnp.pad(values, widths)
        extent = values.shape[axis_dim]
        for offset in range(1, 5):
            upper = lax.slice_in_dim(padded, 4 + offset, 4 + offset + extent, axis=axis_dim)
            lower = lax.slice_in_dim(padded, 4 - offset, 4 - offset + extent, axis=axis_dim)
            total = total + coefficients[offset] * (upper + lower)
    return total

def reference(orbitals, potential):
    grid_potential = to_grid(potential)

    def hamiltonian(values):
        return -0.5 * laplacian(values) + grid_potential * values

    def filter_one(tiles):
        start_values = to_grid(tiles)
        previous = start_values
        current = (hamiltonian(start_values) - centre_value * start_values) / half_range
        for step_index in range(DEG - 1):
            following = 2.0 * (hamiltonian(current) - centre_value * current) / half_range - previous
            previous, current = (current, following)
        return from_grid(current * filter_scale)
    filtered = lax.map(filter_one, orbitals)
    flat = filtered.reshape(NORB, -1)
    total_cells = flat.shape[1]
    identity = jnp.eye(NORB, dtype=jnp.float32)
    current = flat
    lowers = []
    for round_index in range(2):
        gram = jnp.dot(current.astype(jnp.float32), current.T.astype(jnp.float32), precision=lax.Precision.HIGHEST, preferred_element_type=jnp.float32) / total_cells
        lower = jnp.linalg.cholesky(gram)
        inverse = jax.scipy.linalg.solve_triangular(lower, identity, lower=True)
        current = jnp.dot(inverse.astype(jnp.float32), current.astype(jnp.float32), precision=lax.Precision.HIGHEST, preferred_element_type=jnp.float32)
        lowers.append(lower)
    factor = jnp.dot(lowers[0].astype(jnp.float32), lowers[1].astype(jnp.float32), precision=lax.Precision.HIGHEST, preferred_element_type=jnp.float32).T
    return (current.reshape(orbitals.shape), factor)
```

```python
import jax
import jax.numpy as jnp
from jax import lax
from jax.sharding import PartitionSpec as P

DEG = 4


coefficients = (-205.0 / 72.0, 8.0 / 5.0, -1.0 / 5.0, 8.0 / 315.0, -1.0 / 560.0)
centre_value = 9.25
half_range = 4.75
filter_scale = 1.0 / 32.0


def shifted(block, axis, distance):
    devices = range(lax.axis_size(axis))
    route = [(i - distance, i) for i in devices if i - distance in devices]
    return lax.ppermute(block, axis, route)


def padded_along(field_in, axis_dim, stride, tile_count, coordinate):
    extent = field_in.shape[axis_dim]
    if tile_count == 1:
        widths = [(0, 0)] * field_in.ndim
        widths[axis_dim] = (4, 4)
        return jnp.pad(field_in, widths)
    top_layers = lax.slice_in_dim(field_in, extent - 4, extent, axis=axis_dim)
    bottom_layers = lax.slice_in_dim(field_in, 0, 4, axis=axis_dim)
    received = []
    for direction, portion, retain in (
        (1, top_layers, coordinate > 0),
        (-1, bottom_layers, coordinate < tile_count - 1),
    ):
        arrived = shifted(portion, "space", direction * stride)
        received.append(jnp.where(retain, arrived, jnp.zeros_like(arrived)))
    return jnp.concatenate([received[0], field_in, received[1]], axis=axis_dim)


def hamiltonian(field_in, potential, layout):
    total = 3.0 * coefficients[0] * field_in
    for axis_dim, stride, tile_count, coordinate in layout:
        padded = padded_along(field_in, axis_dim, stride, tile_count, coordinate)
        extent = field_in.shape[axis_dim]
        for offset in range(1, 5):
            upper = lax.slice_in_dim(padded, 4 + offset, 4 + offset + extent, axis=axis_dim)
            lower = lax.slice_in_dim(padded, 4 - offset, 4 - offset + extent, axis=axis_dim)
            total = total + coefficients[offset] * (upper + lower)
    return -0.5 * total + potential * field_in


def orthonormalize(flat, reduce_gram, total_cells):
    count_orbs = flat.shape[0]
    identity = jnp.eye(count_orbs, dtype=jnp.float32)
    current = flat
    lowers = []
    for round_index in range(2):
        partial_gram = jnp.dot(
            current, current.T, precision=lax.Precision.HIGHEST, preferred_element_type=jnp.float32
        )
        gram = reduce_gram(partial_gram) / total_cells
        lower = jnp.linalg.cholesky(gram)
        inverse = jax.scipy.linalg.solve_triangular(lower, identity, lower=True)
        current = jnp.dot(
            inverse, current, precision=lax.Precision.HIGHEST, preferred_element_type=jnp.float32
        )
        lowers.append(lower)
    factor = jnp.dot(
        lowers[0], lowers[1], precision=lax.Precision.HIGHEST, preferred_element_type=jnp.float32
    ).T
    return (current, factor)


def shards(orbitals, potential):
    tile_index = lax.axis_index("space")
    layout = (
        (2, 16, lax.axis_size("space") // 16, tile_index // 16),
        (3, 4, 4, tile_index // 4 % 4),
        (4, 1, 4, tile_index % 4),
    )
    previous = orbitals
    current = (hamiltonian(orbitals, potential, layout) - centre_value * orbitals) / half_range
    for step_index in range(DEG - 1):
        following = (
            2.0 * (hamiltonian(current, potential, layout) - centre_value * current) / half_range
            - previous
        )
        previous, current = (current, following)
    filtered = current * filter_scale
    row_share = lax.all_to_all(filtered, "band", split_axis=2, concat_axis=0, tiled=True)
    flat = row_share.reshape(row_share.shape[0], -1)
    total_cells = flat.shape[1] * lax.axis_size("space") * lax.axis_size("band")

    def reduce_everywhere(partial_gram):
        gathered = lax.all_gather(partial_gram, ("space", "band"))
        return jnp.sum(gathered, axis=0)

    ortho, factor = orthonormalize(flat, reduce_everywhere, total_cells)
    basis = lax.all_to_all(
        ortho.reshape(row_share.shape), "band", split_axis=0, concat_axis=2, tiled=True
    )
    return (basis, factor)


def solution(mesh):
    return jax.shard_map(
        shards,
        mesh=mesh,
        in_specs=(P("band", "space", None, None, None), P("space", None, None, None)),
        out_specs=(P("band", "space", None, None, None), P()),
        check_vma=False,
    )
```

```python
import jax
import jax.numpy as jnp
from jax import lax
from jax.sharding import PartitionSpec as P

DEG = 4


coefficients = (-205.0 / 72.0, 8.0 / 5.0, -1.0 / 5.0, 8.0 / 315.0, -1.0 / 560.0)
centre_value = 9.25
half_range = 4.75
filter_scale = 1.0 / 32.0


def shifted(block, axis, distance):
    devices = range(lax.axis_size(axis))
    route = [(i - distance, i) for i in devices if i - distance in devices]
    return lax.ppermute(block, axis, route)


def padded_along(field_in, axis_dim, stride, tile_count, coordinate):
    extent = field_in.shape[axis_dim]
    if tile_count == 1:
        widths = [(0, 0)] * field_in.ndim
        widths[axis_dim] = (4, 4)
        return jnp.pad(field_in, widths)
    top_layers = lax.slice_in_dim(field_in, extent - 4, extent, axis=axis_dim)
    bottom_layers = lax.slice_in_dim(field_in, 0, 4, axis=axis_dim)
    received = []
    for direction, portion, retain in (
        (1, top_layers, coordinate > 0),
        (-1, bottom_layers, coordinate < tile_count - 1),
    ):
        arrived = shifted(portion, "space", direction * stride)
        received.append(jnp.where(retain, arrived, jnp.zeros_like(arrived)))
    return jnp.concatenate([received[0], field_in, received[1]], axis=axis_dim)


def hamiltonian(field_in, potential, layout):
    total = 3.0 * coefficients[0] * field_in
    for axis_dim, stride, tile_count, coordinate in layout:
        padded = padded_along(field_in, axis_dim, stride, tile_count, coordinate)
        extent = field_in.shape[axis_dim]
        for offset in range(1, 5):
            upper = lax.slice_in_dim(padded, 4 + offset, 4 + offset + extent, axis=axis_dim)
            lower = lax.slice_in_dim(padded, 4 - offset, 4 - offset + extent, axis=axis_dim)
            total = total + coefficients[offset] * (upper + lower)
    return -0.5 * total + potential * field_in


def orthonormalize(flat, reduce_gram, total_cells):
    count_orbs = flat.shape[0]
    identity = jnp.eye(count_orbs, dtype=jnp.float32)
    current = flat
    lowers = []
    for round_index in range(2):
        partial_gram = jnp.dot(
            current, current.T, precision=lax.Precision.HIGHEST, preferred_element_type=jnp.float32
        )
        gram = reduce_gram(partial_gram) / total_cells
        lower = jnp.linalg.cholesky(gram)
        inverse = jax.scipy.linalg.solve_triangular(lower, identity, lower=True)
        current = jnp.dot(
            inverse, current, precision=lax.Precision.HIGHEST, preferred_element_type=jnp.float32
        )
        lowers.append(lower)
    factor = jnp.dot(
        lowers[0], lowers[1], precision=lax.Precision.HIGHEST, preferred_element_type=jnp.float32
    ).T
    return (current, factor)


def shards(orbitals, potential):
    tile_index = lax.axis_index("space")
    layout = (
        (2, 16, lax.axis_size("space") // 16, tile_index // 16),
        (3, 4, 4, tile_index // 4 % 4),
        (4, 1, 4, tile_index % 4),
    )
    previous = orbitals
    current = (hamiltonian(orbitals, potential, layout) - centre_value * orbitals) / half_range
    for step_index in range(DEG - 1):
        following = (
            2.0 * (hamiltonian(current, potential, layout) - centre_value * current) / half_range
            - previous
        )
        previous, current = (current, following)
    filtered = current * filter_scale
    row_share = lax.all_to_all(filtered, "band", split_axis=2, concat_axis=0, tiled=True)
    flat = row_share.reshape(row_share.shape[0], -1)
    total_cells = flat.shape[1] * lax.axis_size("space") * lax.axis_size("band")

    def reduce_everywhere(partial_gram):
        total = partial_gram
        for axis in ("band", "space"):
            size = lax.axis_size(axis)
            step = 1
            while step < size:
                route = [(i, i ^ step) for i in range(size)]
                total = total + lax.ppermute(total, axis, route)
                step *= 2
        return total

    ortho, factor = orthonormalize(flat, reduce_everywhere, total_cells)
    basis = lax.all_to_all(
        ortho.reshape(row_share.shape), "band", split_axis=0, concat_axis=2, tiled=True
    )
    return (basis, factor)


def solution(mesh):
    return jax.shard_map(
        shards,
        mesh=mesh,
        in_specs=(P("band", "space", None, None, None), P("space", None, None, None)),
        out_specs=(P("band", "space", None, None, None), P()),
        check_vma=False,
    )
```

```python
import jax
import jax.numpy as jnp
from jax import lax
from jax.sharding import PartitionSpec as P

DEG = 4


coefficients = (-205.0 / 72.0, 8.0 / 5.0, -1.0 / 5.0, 8.0 / 315.0, -1.0 / 560.0)
centre_value = 9.25
half_range = 4.75
filter_scale = 1.0 / 32.0


def shifted(block, axis, distance):
    devices = range(lax.axis_size(axis))
    route = [(i - distance, i) for i in devices if i - distance in devices]
    return lax.ppermute(block, axis, route)


def padded_along(field_in, axis_dim, stride, tile_count, coordinate):
    extent = field_in.shape[axis_dim]
    if tile_count == 1:
        widths = [(0, 0)] * field_in.ndim
        widths[axis_dim] = (4, 4)
        return jnp.pad(field_in, widths)
    top_layers = lax.slice_in_dim(field_in, extent - 4, extent, axis=axis_dim)
    bottom_layers = lax.slice_in_dim(field_in, 0, 4, axis=axis_dim)
    received = []
    for direction, portion, retain in (
        (1, top_layers, coordinate > 0),
        (-1, bottom_layers, coordinate < tile_count - 1),
    ):
        arrived = shifted(portion, "space", direction * stride)
        received.append(jnp.where(retain, arrived, jnp.zeros_like(arrived)))
    return jnp.concatenate([received[0], field_in, received[1]], axis=axis_dim)


def hamiltonian(field_in, potential, layout):
    total = 3.0 * coefficients[0] * field_in
    for axis_dim, stride, tile_count, coordinate in layout:
        padded = padded_along(field_in, axis_dim, stride, tile_count, coordinate)
        extent = field_in.shape[axis_dim]
        for offset in range(1, 5):
            upper = lax.slice_in_dim(padded, 4 + offset, 4 + offset + extent, axis=axis_dim)
            lower = lax.slice_in_dim(padded, 4 - offset, 4 - offset + extent, axis=axis_dim)
            total = total + coefficients[offset] * (upper + lower)
    return -0.5 * total + potential * field_in


def orthonormalize(flat, reduce_gram, total_cells, rows, own_count):
    count_orbs = flat.shape[0]
    identity = jnp.eye(count_orbs, dtype=jnp.float32)
    current = flat
    lowers = []
    for round_index in range(2):
        partial_gram = jnp.dot(
            current, current.T, precision=lax.Precision.HIGHEST, preferred_element_type=jnp.float32
        )
        gram = reduce_gram(partial_gram) / total_cells
        lower = jnp.linalg.cholesky(gram)
        inverse = jax.scipy.linalg.solve_triangular(lower, identity, lower=True)
        if round_index == 1:
            inverse = lax.dynamic_slice_in_dim(inverse, rows, own_count, axis=0)
        current = jnp.dot(
            inverse, current, precision=lax.Precision.HIGHEST, preferred_element_type=jnp.float32
        )
        lowers.append(lower)
    factor = jnp.dot(
        lowers[0], lowers[1], precision=lax.Precision.HIGHEST, preferred_element_type=jnp.float32
    ).T
    return (current, factor)


def shards(orbitals, potential):
    tile_index = lax.axis_index("space")
    layout = (
        (2, 16, lax.axis_size("space") // 16, tile_index // 16),
        (3, 4, 4, tile_index // 4 % 4),
        (4, 1, 4, tile_index % 4),
    )
    previous = orbitals
    current = (hamiltonian(orbitals, potential, layout) - centre_value * orbitals) / half_range
    for step_index in range(DEG - 1):
        following = (
            2.0 * (hamiltonian(current, potential, layout) - centre_value * current) / half_range
            - previous
        )
        previous, current = (current, following)
    filtered = current * filter_scale
    own_count = filtered.shape[0]
    everything = lax.all_gather(filtered, "band", axis=0, tiled=True)
    flat = everything.reshape(everything.shape[0], -1)
    total_cells = flat.shape[1] * lax.axis_size("space")

    def reduce_everywhere(partial_gram):
        total = partial_gram
        size = lax.axis_size("space")
        step = 1
        while step < size:
            route = [(i, i ^ step) for i in range(size)]
            total = total + lax.ppermute(total, "space", route)
            step *= 2
        return total

    rows = lax.axis_index("band") * own_count
    ortho, factor = orthonormalize(flat, reduce_everywhere, total_cells, rows, own_count)
    basis = ortho.reshape(filtered.shape)
    return (basis, factor)


def solution(mesh):
    return jax.shard_map(
        shards,
        mesh=mesh,
        in_specs=(P("band", "space", None, None, None), P("space", None, None, None)),
        out_specs=(P("band", "space", None, None, None), P()),
        check_vma=False,
    )
```

```python
import jax
import jax.numpy as jnp
from jax import lax
from jax.sharding import PartitionSpec as P

DEG = 4


coefficients = (-205.0 / 72.0, 8.0 / 5.0, -1.0 / 5.0, 8.0 / 315.0, -1.0 / 560.0)
centre_value = 9.25
half_range = 4.75
filter_scale = 1.0 / 32.0


def shifted(block, axis, distance):
    devices = range(lax.axis_size(axis))
    route = [(i - distance, i) for i in devices if i - distance in devices]
    return lax.ppermute(block, axis, route)


def padded_along(field_in, axis_dim, stride, tile_count, coordinate):
    extent = field_in.shape[axis_dim]
    if tile_count == 1:
        widths = [(0, 0)] * field_in.ndim
        widths[axis_dim] = (4, 4)
        return jnp.pad(field_in, widths)
    top_layers = lax.slice_in_dim(field_in, extent - 4, extent, axis=axis_dim)
    bottom_layers = lax.slice_in_dim(field_in, 0, 4, axis=axis_dim)
    received = []
    for direction, portion, retain in (
        (1, top_layers, coordinate > 0),
        (-1, bottom_layers, coordinate < tile_count - 1),
    ):
        arrived = shifted(portion, "space", direction * stride)
        received.append(jnp.where(retain, arrived, jnp.zeros_like(arrived)))
    return jnp.concatenate([received[0], field_in, received[1]], axis=axis_dim)


def hamiltonian(field_in, potential, layout):
    total = 3.0 * coefficients[0] * field_in
    for axis_dim, stride, tile_count, coordinate in layout:
        padded = padded_along(field_in, axis_dim, stride, tile_count, coordinate)
        extent = field_in.shape[axis_dim]
        for offset in range(1, 5):
            upper = lax.slice_in_dim(padded, 4 + offset, 4 + offset + extent, axis=axis_dim)
            lower = lax.slice_in_dim(padded, 4 - offset, 4 - offset + extent, axis=axis_dim)
            total = total + coefficients[offset] * (upper + lower)
    return -0.5 * total + potential * field_in


def orthonormalize(flat, reduce_gram, total_cells, rows, own_count):
    count_orbs = flat.shape[0]
    identity = jnp.eye(count_orbs, dtype=jnp.float32)
    current = flat
    lowers = []
    for round_index in range(2):
        partial_gram = jnp.dot(
            current, current.T, precision=lax.Precision.HIGHEST, preferred_element_type=jnp.float32
        )
        gram = reduce_gram(partial_gram) / total_cells
        lower = jnp.linalg.cholesky(gram)
        inverse = jax.scipy.linalg.solve_triangular(lower, identity, lower=True)
        if round_index == 1:
            inverse = lax.dynamic_slice_in_dim(inverse, rows, own_count, axis=0)
        current = jnp.dot(
            inverse, current, precision=lax.Precision.HIGHEST, preferred_element_type=jnp.float32
        )
        lowers.append(lower)
    factor = jnp.dot(
        lowers[0], lowers[1], precision=lax.Precision.HIGHEST, preferred_element_type=jnp.float32
    ).T
    return (current, factor)


def shards(orbitals, potential):
    tile_index = lax.axis_index("space")
    layout = (
        (2, 16, lax.axis_size("space") // 16, tile_index // 16),
        (3, 4, 4, tile_index // 4 % 4),
        (4, 1, 4, tile_index % 4),
    )
    previous = orbitals
    current = (hamiltonian(orbitals, potential, layout) - centre_value * orbitals) / half_range
    for step_index in range(DEG - 1):
        following = (
            2.0 * (hamiltonian(current, potential, layout) - centre_value * current) / half_range
            - previous
        )
        previous, current = (current, following)
    filtered = current * filter_scale
    own_count = filtered.shape[0]
    if lax.axis_size("band") == 2:
        other = lax.ppermute(filtered, "band", [(0, 1), (1, 0)])
        first_band = lax.axis_index("band") == 0
        everything = jnp.concatenate(
            [jnp.where(first_band, filtered, other), jnp.where(first_band, other, filtered)], axis=0
        )
    else:
        everything = lax.all_gather(filtered, "band", axis=0, tiled=True)
    flat = everything.reshape(everything.shape[0], -1)
    total_cells = flat.shape[1] * lax.axis_size("space")

    def reduce_everywhere(partial_gram):
        total = partial_gram
        size = lax.axis_size("space")
        step = 1
        while step < size:
            route = [(i, i ^ step) for i in range(size)]
            total = total + lax.ppermute(total, "space", route)
            step *= 2
        return total

    rows = lax.axis_index("band") * own_count
    ortho, factor = orthonormalize(flat, reduce_everywhere, total_cells, rows, own_count)
    basis = ortho.reshape(filtered.shape)
    return (basis, factor)


def solution(mesh):
    return jax.shard_map(
        shards,
        mesh=mesh,
        in_specs=(P("band", "space", None, None, None), P("space", None, None, None)),
        out_specs=(P("band", "space", None, None, None), P()),
        check_vma=False,
    )
```

```python
import jax
import jax.numpy as jnp
from jax import lax
from jax.sharding import PartitionSpec as P

DEG = 4


coefficients = (-205.0 / 72.0, 8.0 / 5.0, -1.0 / 5.0, 8.0 / 315.0, -1.0 / 560.0)
centre_value = 9.25
half_range = 4.75
filter_scale = 1.0 / 32.0


def shifted(block, axis, distance):
    devices = range(lax.axis_size(axis))
    route = [(i - distance, i) for i in devices if i - distance in devices]
    return lax.ppermute(block, axis, route)


def padded_along(field_in, axis_dim, stride, tile_count, coordinate):
    extent = field_in.shape[axis_dim]
    if tile_count == 1:
        widths = [(0, 0)] * field_in.ndim
        widths[axis_dim] = (4, 4)
        return jnp.pad(field_in, widths)
    top_layers = lax.slice_in_dim(field_in, extent - 4, extent, axis=axis_dim)
    bottom_layers = lax.slice_in_dim(field_in, 0, 4, axis=axis_dim)
    received = []
    for direction, portion, retain in (
        (1, top_layers, coordinate > 0),
        (-1, bottom_layers, coordinate < tile_count - 1),
    ):
        arrived = shifted(portion, "space", direction * stride)
        received.append(jnp.where(retain, arrived, jnp.zeros_like(arrived)))
    return jnp.concatenate([received[0], field_in, received[1]], axis=axis_dim)


def hamiltonian(field_in, potential, layout):
    total = 3.0 * coefficients[0] * field_in
    for axis_dim, stride, tile_count, coordinate in layout:
        padded = padded_along(field_in, axis_dim, stride, tile_count, coordinate)
        extent = field_in.shape[axis_dim]
        for offset in range(1, 5):
            upper = lax.slice_in_dim(padded, 4 + offset, 4 + offset + extent, axis=axis_dim)
            lower = lax.slice_in_dim(padded, 4 - offset, 4 - offset + extent, axis=axis_dim)
            total = total + coefficients[offset] * (upper + lower)
    return -0.5 * total + potential * field_in


def orthonormalize(flat, reduce_gram, total_cells, rows, own_count):
    count_orbs = flat.shape[0]
    identity = jnp.eye(count_orbs, dtype=jnp.float32)
    current = flat
    lowers = []
    for round_index in range(2):
        partial_gram = jnp.tensordot(
            current, current, axes=(tuple(range(1, current.ndim)),) * 2,
            precision=lax.Precision.HIGHEST, preferred_element_type=jnp.float32,
        )
        gram = reduce_gram(partial_gram) / total_cells
        lower = jnp.linalg.cholesky(gram)
        inverse = jax.scipy.linalg.solve_triangular(lower, identity, lower=True)
        if round_index == 1:
            inverse = lax.dynamic_slice_in_dim(inverse, rows, own_count, axis=0)
        current = jnp.tensordot(
            inverse, current, axes=1, precision=lax.Precision.HIGHEST, preferred_element_type=jnp.float32
        )
        lowers.append(lower)
    factor = jnp.dot(
        lowers[0], lowers[1], precision=lax.Precision.HIGHEST, preferred_element_type=jnp.float32
    ).T
    return (current, factor)


def shards(orbitals, potential):
    tile_index = lax.axis_index("space")
    layout = (
        (2, 16, lax.axis_size("space") // 16, tile_index // 16),
        (3, 4, 4, tile_index // 4 % 4),
        (4, 1, 4, tile_index % 4),
    )
    previous = orbitals
    current = (hamiltonian(orbitals, potential, layout) - centre_value * orbitals) / half_range
    for step_index in range(DEG - 1):
        following = (
            2.0 * (hamiltonian(current, potential, layout) - centre_value * current) / half_range
            - previous
        )
        previous, current = (current, following)
    filtered = current * filter_scale
    own_count = filtered.shape[0]
    if lax.axis_size("band") == 2:
        other = lax.ppermute(filtered, "band", [(0, 1), (1, 0)])
        first_band = lax.axis_index("band") == 0
        everything = jnp.concatenate(
            [jnp.where(first_band, filtered, other), jnp.where(first_band, other, filtered)], axis=0
        )
    else:
        everything = lax.all_gather(filtered, "band", axis=0, tiled=True)
    flat = everything
    total_cells = everything[0].size * lax.axis_size("space")

    def reduce_everywhere(partial_gram):
        total = partial_gram
        size = lax.axis_size("space")
        step = 1
        while step < size:
            route = [(i, i ^ step) for i in range(size)]
            total = total + lax.ppermute(total, "space", route)
            step *= 2
        return total

    rows = lax.axis_index("band") * own_count
    ortho, factor = orthonormalize(flat, reduce_everywhere, total_cells, rows, own_count)
    basis = ortho.reshape(filtered.shape)
    return (basis, factor)


def solution(mesh):
    return jax.shard_map(
        shards,
        mesh=mesh,
        in_specs=(P("band", "space", None, None, None), P("space", None, None, None)),
        out_specs=(P("band", "space", None, None, None), P()),
        check_vma=False,
    )
```

```python
import jax
import jax.numpy as jnp
from jax import lax
from jax.sharding import PartitionSpec as P

DEG = 4


coefficients = (-205.0 / 72.0, 8.0 / 5.0, -1.0 / 5.0, 8.0 / 315.0, -1.0 / 560.0)
centre_value = 9.25
half_range = 4.75
filter_scale = 1.0 / 32.0


def shifted(block, axis, distance):
    devices = range(lax.axis_size(axis))
    route = [(i - distance, i) for i in devices if i - distance in devices]
    return lax.ppermute(block, axis, route)


def padded_along(field_in, axis_dim, stride, tile_count, coordinate):
    extent = field_in.shape[axis_dim]
    if tile_count == 1:
        widths = [(0, 0)] * field_in.ndim
        widths[axis_dim] = (4, 4)
        return jnp.pad(field_in, widths)
    top_layers = lax.slice_in_dim(field_in, extent - 4, extent, axis=axis_dim)
    bottom_layers = lax.slice_in_dim(field_in, 0, 4, axis=axis_dim)
    received = []
    devices = range(lax.axis_size("space"))
    for direction, portion in ((1, top_layers), (-1, bottom_layers)):
        distance = direction * stride
        route = [
            (i - distance, i)
            for i in devices
            if i - distance in devices and 0 <= (i // stride) % tile_count - direction < tile_count
        ]
        received.append(lax.ppermute(portion, "space", route))
    return jnp.concatenate([received[0], field_in, received[1]], axis=axis_dim)


def hamiltonian(field_in, potential, layout):
    total = 3.0 * coefficients[0] * field_in
    for axis_dim, stride, tile_count, coordinate in layout:
        padded = padded_along(field_in, axis_dim, stride, tile_count, coordinate)
        extent = field_in.shape[axis_dim]
        for offset in range(1, 5):
            upper = lax.slice_in_dim(padded, 4 + offset, 4 + offset + extent, axis=axis_dim)
            lower = lax.slice_in_dim(padded, 4 - offset, 4 - offset + extent, axis=axis_dim)
            total = total + coefficients[offset] * (upper + lower)
    return -0.5 * total + potential * field_in


def orthonormalize(flat, reduce_gram, total_cells, rows, own_count):
    count_orbs = flat.shape[0]
    identity = jnp.eye(count_orbs, dtype=jnp.float32)
    current = flat
    lowers = []
    for round_index in range(2):
        partial_gram = jnp.tensordot(
            current, current, axes=(tuple(range(1, current.ndim)),) * 2,
            precision=lax.Precision.HIGHEST, preferred_element_type=jnp.float32,
        )
        gram = reduce_gram(partial_gram) / total_cells
        lower = jnp.linalg.cholesky(gram)
        inverse = jax.scipy.linalg.solve_triangular(lower, identity, lower=True)
        if round_index == 1:
            inverse = lax.dynamic_slice_in_dim(inverse, rows, own_count, axis=0)
        current = jnp.tensordot(
            inverse, current, axes=1, precision=lax.Precision.HIGHEST, preferred_element_type=jnp.float32
        )
        lowers.append(lower)
    factor = jnp.dot(
        lowers[0], lowers[1], precision=lax.Precision.HIGHEST, preferred_element_type=jnp.float32
    ).T
    return (current, factor)


def shards(orbitals, potential):
    tile_index = lax.axis_index("space")
    layout = (
        (2, 16, lax.axis_size("space") // 16, tile_index // 16),
        (3, 4, 4, tile_index // 4 % 4),
        (4, 1, 4, tile_index % 4),
    )
    previous = orbitals
    current = (hamiltonian(orbitals, potential, layout) - centre_value * orbitals) / half_range
    for step_index in range(DEG - 1):
        following = (
            2.0 * (hamiltonian(current, potential, layout) - centre_value * current) / half_range
            - previous
        )
        previous, current = (current, following)
    filtered = current * filter_scale
    own_count = filtered.shape[0]
    if lax.axis_size("band") == 2:
        other = lax.ppermute(filtered, "band", [(0, 1), (1, 0)])
        first_band = lax.axis_index("band") == 0
        everything = jnp.concatenate(
            [jnp.where(first_band, filtered, other), jnp.where(first_band, other, filtered)], axis=0
        )
    else:
        everything = lax.all_gather(filtered, "band", axis=0, tiled=True)
    flat = everything
    total_cells = everything[0].size * lax.axis_size("space")

    def reduce_everywhere(partial_gram):
        total = partial_gram
        size = lax.axis_size("space")
        step = 1
        while step < size:
            route = [(i, i ^ step) for i in range(size)]
            total = total + lax.ppermute(total, "space", route)
            step *= 2
        return total

    rows = lax.axis_index("band") * own_count
    ortho, factor = orthonormalize(flat, reduce_everywhere, total_cells, rows, own_count)
    basis = ortho.reshape(filtered.shape)
    return (basis, factor)


def solution(mesh):
    return jax.shard_map(
        shards,
        mesh=mesh,
        in_specs=(P("band", "space", None, None, None), P("space", None, None, None)),
        out_specs=(P("band", "space", None, None, None), P()),
        check_vma=False,
    )
```
